32 devices in a mesh: group: 2 (over x), branch: 8 (over z, y), expert: 2 (over core).
Axes of the slice: x: 2, y: 2, z: 4, core: 2. Of those that a mesh axis runs over, the one named last changes fastest.
Arguments:
- latent_cache: bfloat16 [16, 2048, 512], P(('group', 'branch'), 'expert'), parts along dimension 0, may hold values from -4 to 4
- rope_cache: bfloat16 [16, 256, 512], P(('group', 'branch'), 'expert'), parts along dimension 0, may hold values from -4 to 4
- q_latent: bfloat16 [256, 2, 128, 512], P(('group', 'branch', 'expert')), parts along dimension 0, may hold values from -4.8 to 4.8
- q_rope: bfloat16 [256, 2, 8192], P(('group', 'branch', 'expert')), parts along dimension 0, may hold values from -192 to 192
- new_latent: bfloat16 [256, 2, 512], P(('group', 'branch', 'expert')), parts along dimension 0, may hold values from -4 to 4
- new_rope: bfloat16 [256, 2, 64], P(('group', 'branch', 'expert')), parts along dimension 0, may hold values from -4.2 to 4.2
- branch_slot: int32 [256], P(('group', 'branch', 'expert')), parts along dimension 0, may hold values from 0 to 7, as said below
- moe_input: bfloat16 [256, 2, 7168], P(('group', 'branch', 'expert')), parts along dimension 0, may hold values from -6 to 6
- routes: int32 [256, 2, 8], P(('group', 'branch', 'expert')), parts along dimension 0, may hold values from 0 to 255, as said below
- route_gate: float32 [256, 2, 8], P(('group', 'branch', 'expert')), parts along dimension 0, may hold values from 0.05 to 0.6
- w_gate: bfloat16 [16, 7168, 128], P(('branch', 'expert')), may hold values from -0.0625 to 0.0625
- w_up: bfloat16 [16, 7168, 128], P(('branch', 'expert')), may hold values from -0.0625 to 0.0625
- w_down: bfloat16 [16, 128, 7168], P(('branch', 'expert')), may hold values from -0.1875 to 0.1875
Outputs:
- attended: bfloat16 [256, 2, 128, 512], P(('group', 'branch', 'expert')), parts along dimension 0
- moe_out: bfloat16 [256, 2, 7168], P(('group', 'branch', 'expert')), parts along dimension 0
The draws below stay inside these ranges and needn't reach their ends.
There are 2 independent parts, one for each index of `group`. The reference program is written for one: setup_inputs(seed, part) draws one part's arguments, and reference() takes and returns one part's arrays. A program takes and returns all parts, laid end to end along the dimension named above; an argument that names none is the same for every part. Nothing has to cross between parts.
Inputs may be any that keep to these rules, and one draw needn't show every extreme that they name: `branch_slot`: among the 8 tokens of one device every number from 0 to 7 stands exactly once. `routes`: each row (a token at a step) names 8 different experts, at most one of them below 2; within the 16 rows of one device no expert below 2 is named more than 2 times, and some one exactly 2 times.
All inputs are finite; a program needn't handle non-finite values.
Results may differ from the reference program's by a relative error of at most 0.0057.
Values may be sent and summed in bfloat16 or wider, within the bound.
A program may use at most 192 MiB of HBM per device.

```python
import math
import jax
import jax.numpy as jnp
from jax import lax

D = 7168
HEADS = 128
LAT = 512
ROPE = 64
ALL_EXPERTS = 256
EXP_HID = 1024
SHARDS = 8
TOPK = 8
STEPS = 2
BRANCHES = 16
BLOCK = 8
LEN = 2048
OUTLINES = 8
TOKENS = 128
EXPERTS = 2
CAP = 2


def draw_branch_slot(key, part):
    devices = TOKENS // BLOCK
    scores = jax.random.randint(jax.random.fold_in(key, 11), (devices, BLOCK), 0, 1 << 20)
    scores = scores * BLOCK + jnp.arange(BLOCK, dtype=jnp.int32)[None, :]
    return jnp.argsort(scores, axis=1).astype(jnp.int32).reshape(TOKENS)


def draw_routes(key, part):
    devices = TOKENS // BLOCK
    row_count = STEPS * BLOCK
    others = ALL_EXPERTS - EXPERTS
    keys = jax.random.split(jax.random.fold_in(key, 37), 5)
    scores = jax.random.randint(keys[0], (devices, row_count, others), 0, 1 << 20)
    scores = scores * others + jnp.arange(others, dtype=jnp.int32)[None, None, :]
    unused, picks = lax.top_k(scores, TOPK)
    picks = (picks % others + EXPERTS).astype(jnp.int32)
    order_scores = jax.random.randint(keys[1], (devices, EXPERTS), 0, 1 << 20) * EXPERTS + jnp.arange(EXPERTS, dtype=jnp.int32)[None, :]
    expert_order = jnp.argsort(order_scores, axis=1).astype(jnp.int32)
    row_scores = jax.random.randint(keys[2], (devices, row_count), 0, 1 << 20) * row_count + jnp.arange(row_count, dtype=jnp.int32)[None, :]
    row_order = jnp.argsort(row_scores, axis=1).astype(jnp.int32)
    rank = jnp.argsort(row_order, axis=1).astype(jnp.int32)
    pair = rank // CAP
    kept = (pair < EXPERTS) & ((rank < CAP) | (jax.random.randint(keys[3], (devices, row_count), 0, 8) < 7))
    computed = jnp.take_along_axis(expert_order, jnp.minimum(pair, EXPERTS - 1), axis=1)
    where_slot = jax.random.randint(keys[4], (devices, row_count), 0, TOPK)
    column = jnp.arange(TOPK, dtype=jnp.int32)[None, None, :]
    replace = kept[:, :, None] & (column == where_slot[:, :, None])
    chosen = jnp.where(replace, computed[:, :, None], picks)
    return chosen.reshape(TOKENS, STEPS, TOPK).astype(jnp.int32)


def shared_draws(key, part):
    keys = jax.random.split(jax.random.fold_in(key, 23), 5)
    rope = jnp.clip(jax.random.normal(keys[0], (OUTLINES, LEN, ROPE), jnp.float32), -4.0, 4.0)
    rope_new = jnp.clip(jax.random.normal(keys[1], (TOKENS, STEPS, ROPE), jnp.float32), -4.0, 4.0)
    latent_new = jnp.clip(jax.random.normal(keys[2], (TOKENS, STEPS, LAT), jnp.float32), -4.0, 4.0)
    query_rope = jnp.clip(jax.random.normal(keys[3], (TOKENS, STEPS, HEADS, ROPE), jnp.float32), -4.0, 4.0)
    query_lat = jnp.clip(jax.random.normal(keys[4], (TOKENS, STEPS, HEADS, LAT), jnp.float32), -4.0, 4.0)
    query_lat = query_lat + 0.2 * latent_new[:, :, None, :]
    return (rope, rope_new, latent_new, query_rope, query_lat)


def draw_rope_cache(key, part):
    return shared_draws(key, part)[0].reshape(OUTLINES, LEN // 8, 8 * ROPE).astype(jnp.bfloat16)


def draw_new_rope(key, part):
    return shared_draws(key, part)[1].astype(jnp.bfloat16)


def draw_new_latent(key, part):
    return shared_draws(key, part)[2].astype(jnp.bfloat16)


def draw_q_rope(key, part):
    return shared_draws(key, part)[3].reshape(TOKENS, STEPS, HEADS * ROPE).astype(jnp.bfloat16)


def draw_q_latent(key, part):
    return shared_draws(key, part)[4].astype(jnp.bfloat16)


def steps_of(key, dims, pieces, low, largest):
    level = 1.0
    for dim, blocks in pieces:
        heights = jax.random.uniform(jax.random.fold_in(jax.random.fold_in(key, 6), dim), (blocks,), jnp.float32, low / len(pieces), largest / len(pieces))
        level = level * jnp.repeat(jnp.exp(heights), dims[dim] // blocks).reshape((-1,) + (1,) * (len(dims) - 1 - dim))
    return level


def normal_values(rng, dims, scale, limit, shards=(), held_as=jnp.bfloat16):
    gain = steps_of(rng, dims, shards, -0.22, 0.18) if shards else 1.0
    drawn = jax.random.normal(rng, dims, jnp.float32) * scale * gain
    return jnp.minimum(jnp.maximum(drawn, -limit), limit).astype(held_as)


def setup_inputs(seed: int = 0, part: int = 0) -> dict:
    key_list = jax.random.split(jax.random.key(seed), 14)
    part_splits = jax.random.split(jax.random.fold_in(key_list[13], part), 14)
    return {
        "latent_cache": normal_values(part_splits[0], (OUTLINES, LEN, LAT), 1.0, 4.0, ((0, 8), (1, 2))),
        "rope_cache": draw_rope_cache(jax.random.fold_in(jax.random.fold_in(key_list[13], part), 71), part),
        "q_latent": draw_q_latent(jax.random.fold_in(jax.random.fold_in(key_list[13], part), 71), part),
        "q_rope": draw_q_rope(jax.random.fold_in(jax.random.fold_in(key_list[13], part), 71), part),
        "new_latent": draw_new_latent(jax.random.fold_in(jax.random.fold_in(key_list[13], part), 71), part),
        "new_rope": draw_new_rope(jax.random.fold_in(jax.random.fold_in(key_list[13], part), 71), part),
        "branch_slot": draw_branch_slot(jax.random.fold_in(jax.random.fold_in(key_list[13], part), 71), part),
        "moe_input": normal_values(part_splits[7], (TOKENS, STEPS, D), 1.0, 6.0, ((0, 16),)),
        "routes": draw_routes(jax.random.fold_in(jax.random.fold_in(key_list[13], part), 71), part),
        "route_gate": jnp.clip(jnp.exp(math.log(0.6) - 2.4849067 * jax.random.uniform(part_splits[9], (TOKENS, STEPS, TOPK), jnp.float32) ** steps_of(part_splits[9], (TOKENS, STEPS, TOPK), ((0, 16),), -0.2, 0.2)), 0.05, 0.6),
        "w_gate": normal_values(key_list[10], (EXPERTS * SHARDS, D, EXP_HID // SHARDS), D ** -0.5, 0.0625, ((0, 16),)),
        "w_up": normal_values(key_list[11], (EXPERTS * SHARDS, D, EXP_HID // SHARDS), D ** -0.5, 0.0625, ((0, 16),)),
        "w_down": normal_values(key_list[12], (EXPERTS * SHARDS, EXP_HID // SHARDS, D), EXP_HID ** -0.5, 0.1875, ((0, 16),)),
    }


softmax_scale = 192.0 ** -0.5


def cache_partial(query_lat, query_rope, keys_lat, keys_rope):
    highest = lax.Precision.HIGHEST
    scores = jnp.einsum("tshc,pc->tshp", query_lat, keys_lat, precision=highest)
    scores = scores + jnp.einsum("tshr,pr->tshp", query_rope, keys_rope, precision=highest)
    scores = scores * softmax_scale
    cache_peak = jnp.max(scores, axis=-1)
    exponent = jnp.exp(scores - cache_peak[..., None])
    totals = jnp.sum(exponent, axis=-1)
    weights = lax.optimization_barrier(exponent.astype(jnp.bfloat16)).astype(jnp.float32)
    summed = jnp.einsum("tshp,pc->tshc", weights, keys_lat, precision=highest)
    return cache_peak, totals, summed


def expert_ffn(packed):
    arrived, gate_matrix, up_matrix, down_matrix = packed
    highest = lax.Precision.HIGHEST
    inputs = arrived.astype(jnp.float32)
    gate_value = jnp.einsum("rd,jdh->jrh", inputs, gate_matrix.astype(jnp.float32), precision=highest)
    lifted = jnp.einsum("rd,jdh->jrh", inputs, up_matrix.astype(jnp.float32), precision=highest)
    hidden = lax.optimization_barrier((jax.nn.silu(gate_value) * lifted).astype(jnp.bfloat16)).astype(jnp.float32)
    parts = jnp.einsum("jrh,jhd->jrd", hidden, down_matrix.astype(jnp.float32), precision=highest)
    parts = lax.optimization_barrier(parts.astype(jnp.bfloat16)).astype(jnp.float32)
    return jnp.sum(parts, axis=0)


def reference(latent_cache, rope_cache, q_latent, q_rope, new_latent, new_rope, branch_slot, moe_input, routes, route_gate, w_gate, w_up, w_down):
    highest = lax.Precision.HIGHEST
    token_ids = jnp.arange(TOKENS, dtype=jnp.int32)
    outline = (BLOCK * (token_ids // (BRANCHES * BLOCK)) + branch_slot).astype(jnp.int32)
    members = jnp.argsort(outline, stable=True).astype(jnp.int32).reshape(OUTLINES, BRANCHES)
    query_rope_all = q_rope.reshape(TOKENS, STEPS, HEADS, ROPE)
    rope_keys = rope_cache.reshape(OUTLINES, LEN, ROPE)

    def per_outline(outline_index):
        chosen = members[outline_index]
        query_lat = jnp.take(q_latent, chosen, axis=0).astype(jnp.float32)
        query_rope = jnp.take(query_rope_all, chosen, axis=0).astype(jnp.float32)
        keys_lat = latent_cache[outline_index].astype(jnp.float32)
        keys_rope = rope_keys[outline_index].astype(jnp.float32)
        return cache_partial(query_lat, query_rope, keys_lat, keys_rope)

    cache_peak, totals, summed = lax.map(per_outline, jnp.arange(OUTLINES, dtype=jnp.int32))
    position_of = jnp.zeros((TOKENS,), jnp.int32).at[members.reshape(-1)].set(token_ids)
    cache_peak = jnp.take(cache_peak.reshape((TOKENS,) + cache_peak.shape[2:]), position_of, axis=0)
    totals = jnp.take(totals.reshape((TOKENS,) + totals.shape[2:]), position_of, axis=0)
    summed = jnp.take(summed.reshape((TOKENS,) + summed.shape[2:]), position_of, axis=0)
    cache_out = lax.optimization_barrier((summed / totals[..., None]).astype(jnp.bfloat16)).astype(jnp.float32)
    cache_lse = cache_peak + jnp.log(totals)

    latent_own = new_latent.astype(jnp.float32)
    own_scores = jnp.einsum("tshc,tjc->tshj", q_latent.astype(jnp.float32), latent_own, precision=highest)
    own_scores = own_scores + jnp.einsum("tshr,tjr->tshj", query_rope_all.astype(jnp.float32), new_rope.astype(jnp.float32), precision=highest)
    own_scores = own_scores * softmax_scale
    causal = (jnp.arange(STEPS)[None, :] <= jnp.arange(STEPS)[:, None])[None, :, None, :]
    own_peak = jnp.max(jnp.where(causal, own_scores, -1e30), axis=-1)
    own_weight = jnp.where(causal, jnp.exp(own_scores - own_peak[..., None]), 0.0)
    own_total = jnp.sum(own_weight, axis=-1)
    own_sum = jnp.einsum("tshj,tjc->tshc", own_weight, latent_own, precision=highest)
    top_value = jnp.maximum(cache_lse, own_peak)
    factor = jnp.exp(cache_lse - top_value)
    own_factor = jnp.exp(own_peak - top_value)
    numerator = factor[..., None] * cache_out + own_factor[..., None] * own_sum
    denominator = factor + own_factor * own_total
    attended = (numerator / denominator[..., None]).astype(jnp.bfloat16)

    devices = TOKENS // BLOCK
    per_device = STEPS * BLOCK * TOPK
    slot_total = EXPERTS * devices * CAP
    flat_routes = routes.reshape(devices, per_device).astype(jnp.int32)
    inside = flat_routes < EXPERTS
    onehot = (flat_routes[:, :, None] == jnp.arange(EXPERTS, dtype=jnp.int32)[None, None, :]).astype(jnp.int32)
    position = jnp.sum((jnp.cumsum(onehot, axis=1) - onehot) * onehot, axis=2)
    slot_index = flat_routes * (devices * CAP) + jnp.arange(devices, dtype=jnp.int32)[:, None] * CAP + position
    slot_index = jnp.where(inside, slot_index, slot_total).reshape(-1).astype(jnp.int32)
    rows_flat = moe_input.reshape(TOKENS * STEPS, D)
    source = jnp.repeat(rows_flat, TOPK, axis=0)
    buffer = jnp.zeros((slot_total, D), jnp.bfloat16).at[slot_index].set(source, mode="drop")
    hid_block = EXP_HID // SHARDS
    outputs = lax.map(expert_ffn, (buffer.reshape(EXPERTS, devices * CAP, D),
                                   w_gate.reshape(EXPERTS, SHARDS, D, hid_block),
                                   w_up.reshape(EXPERTS, SHARDS, D, hid_block),
                                   w_down.reshape(EXPERTS, SHARDS, hid_block, D)))
    safe_index = jnp.minimum(slot_index, slot_total - 1).astype(jnp.int32)
    picked = jnp.take(outputs.reshape(-1, D), safe_index, axis=0).reshape(TOKENS * STEPS, TOPK, D)
    gate_used = jnp.where(inside.reshape(TOKENS * STEPS, TOPK), route_gate.reshape(TOKENS * STEPS, TOPK), 0.0)
    combined = jnp.sum(gate_used[:, :, None] * picked, axis=1)
    moe_out = combined.astype(jnp.bfloat16).reshape(TOKENS, STEPS, D)
    return attended, moe_out
```

```python
import functools

import jax
import jax.numpy as jnp
from jax import lax
from jax.experimental import pallas as pl
from jax.experimental.pallas import tpu as pltpu
from jax.sharding import PartitionSpec as P

SHARDS = 8
CAP = 2
HALF = 4
CHUNKS = 4

softmax_scale = 192.0 ** (-0.5)


def flipped(r, x, bits):
    out = r - r % (1 << bits)
    for j in range(bits):
        out = out + (((r // (1 << j)) + (x // (1 << j))) % 2) * (1 << j)
    return out


def attend_kernel(
    ordering_ref,
    target_ref,
    q_ref,
    rope_ref,
    new_ref,
    keys_ref,
    krope_ref,
    out_ref,
    q_send,
    rope_send,
    new_send,
    q_in,
    rope_in,
    new_in,
    keys,
    kpack,
    kdup,
    result,
    answers,
    sib_send,
    sib_recv,
    part_send,
    part_recv,
    fwd_send,
    fwd_recv,
    query_send,
    query_recv,
    ans_send,
    ans_recv,
):
    branch = lax.axis_index("branch")
    core = lax.axis_index("expert")
    tok = q_ref.shape[0]
    rows = q_ref.shape[1]
    half_len = keys_ref.shape[0]
    packed_len = krope_ref.shape[0]
    heads = rope_ref.shape[1]
    lanes = rope_ref.shape[2]
    step_rows = half_len // CHUNKS
    pack_rows = packed_len // CHUNKS

    def place(b, c):
        return {"branch": b, "expert": c}

    sibling = place(branch, 1 - core)
    partner = place(flipped(branch, HALF, 3), core)

    def peer(x):
        return place(flipped(branch, x % HALF, 3), core)

    barrier = pltpu.get_barrier_semaphore()
    for other in [sibling, partner] + [peer(j) for j in range(1, HALF)]:
        pl.semaphore_signal(
            barrier, inc=1, device_id=other, device_id_type=pl.DeviceIdType.MESH
        )
    pl.semaphore_wait(barrier, 2 + HALF - 1)

    def remote(src, dst, send, recv, where):
        return pltpu.make_async_remote_copy(
            src_ref=src,
            dst_ref=dst,
            send_sem=send,
            recv_sem=recv,
            device_id=where,
            device_id_type=pl.DeviceIdType.MESH,
        )

    def sib_copies():
        return [
            remote(keys_ref, keys.at[0], sib_send.at[0], sib_recv.at[0], sibling),
            remote(krope_ref, kpack.at[0], sib_send.at[1], sib_recv.at[1], sibling),
        ]

    def part_copies(c):
        big = pl.ds(c * step_rows, step_rows)
        small = pl.ds(c * pack_rows, pack_rows)
        return [
            remote(
                keys_ref.at[big], keys.at[1, big], part_send.at[0, c], part_recv.at[0, c], partner
            ),
            remote(
                krope_ref.at[small],
                kpack.at[1, small],
                part_send.at[1, c],
                part_recv.at[1, c],
                partner,
            ),
        ]

    def fwd_copies(c):
        big = pl.ds(c * step_rows, step_rows)
        small = pl.ds(c * pack_rows, pack_rows)
        return [
            remote(
                keys.at[1, big], keys.at[2, big], fwd_send.at[0, c], fwd_recv.at[0, c], sibling
            ),
            remote(
                kpack.at[1, small], kpack.at[2, small], fwd_send.at[1, c], fwd_recv.at[1, c], sibling
            ),
        ]

    def query_copies(x):
        where = peer(x)
        return [
            remote(q_send.at[x], q_in.at[x], query_send.at[0, x], query_recv.at[0, x], where),
            remote(rope_send.at[x], rope_in.at[x], query_send.at[1, x], query_recv.at[1, x], where),
            remote(new_send.at[x], new_in.at[x], query_send.at[2, x], query_recv.at[2, x], where),
        ]

    def answer_copy(x):
        return remote(result.at[x], answers.at[x], ans_send.at[x], ans_recv.at[x], peer(x))

    def gather(x, to_q, to_rope, to_new):
        at = ordering_ref[x]
        to_q[x] = q_ref[at]
        to_rope[x] = rope_ref[at]
        to_new[x] = new_ref[at]

    for copy in sib_copies():
        copy.start()
    order = [2, 3, 6, 7]
    for c in range(CHUNKS):
        for copy in part_copies(c):
            copy.start()
        x = order[c]
        gather(x, q_send, rope_send, new_send)
        for copy in query_copies(x):
            copy.start()
        if c % 2 == 0:
            y = (1, 5)[c // 2]
            gather(y, q_send, rope_send, new_send)
            for copy in query_copies(y):
                copy.start()
    for x in (0, HALF):
        gather(x, q_in, rope_in, new_in)

    lane = lax.broadcasted_iota(jnp.int32, (packed_len, lanes), 1)
    low = lane < lanes // 2

    def spread(packed, slot):
        values = packed.astype(jnp.float32)
        turned = pltpu.roll(values, lanes // 2, 1)
        kdup[slot, pl.ds(0, packed_len)] = jnp.where(low, values, turned).astype(jnp.bfloat16)
        kdup[slot, pl.ds(packed_len, packed_len)] = jnp.where(low, turned, values).astype(
            jnp.bfloat16
        )

    nt = (((1,), (1,)), ((), ()))
    nn = (((1,), (0,)), ((), ()))
    head_low = lax.broadcasted_iota(jnp.int32, (heads, lanes), 1) < lanes // 2
    second = lax.broadcasted_iota(jnp.int32, (rows, 1), 0) >= heads

    def attend(x, first_keys, first_rope, other_keys, other_rope):
        q = q_in[x]
        packed = rope_in[x].astype(jnp.float32)
        qr = jnp.concatenate(
            [jnp.where(head_low, packed, 0.0), jnp.where(head_low, 0.0, packed)], axis=0
        ).astype(jnp.bfloat16)
        fresh = new_in[x]
        lat = q.shape[1]

        def score(k, kr):
            return lax.dot_general(
                q, k, nt, preferred_element_type=jnp.float32
            ) + lax.dot_general(qr, kr, nt, preferred_element_type=jnp.float32)

        own = score(fresh[:, :lat], fresh[:, lat:])
        own0 = own[:, 0:1]
        own1 = jnp.where(second, own[:, 1:2], -1e30)
        s0 = score(first_keys[...], first_rope[...])
        s1 = score(other_keys[...], other_rope[...])
        top = jnp.maximum(jnp.max(s0, axis=1, keepdims=True), jnp.max(s1, axis=1, keepdims=True))
        top = jnp.maximum(top, jnp.maximum(own0, own1))
        p0 = jnp.exp((s0 - top) * softmax_scale)
        p1 = jnp.exp((s1 - top) * softmax_scale)
        w0 = jnp.exp((own0 - top) * softmax_scale)
        w1 = jnp.where(second, jnp.exp((own1 - top) * softmax_scale), 0.0)
        total = jnp.sum(p0, axis=1, keepdims=True) + jnp.sum(p1, axis=1, keepdims=True) + w0 + w1
        summed = lax.dot_general(
            p0.astype(jnp.bfloat16), first_keys[...], nn, preferred_element_type=jnp.float32
        ) + lax.dot_general(
            p1.astype(jnp.bfloat16), other_keys[...], nn, preferred_element_type=jnp.float32
        )
        entries = fresh[:, :lat].astype(jnp.float32)
        summed = summed + w0 * entries[0:1] + w1 * entries[1:2]
        return (summed / total).astype(jnp.bfloat16)

    def run(start, *cache):
        answers[start] = attend(start, *cache)

        def body(x, carry):
            for copy in query_copies(x):
                copy.wait_recv()
            result[x] = attend(x, *cache)
            answer_copy(x).start()
            return carry

        lax.fori_loop(start + 1, start + HALF, body, 0)

    spread(krope_ref[...], 0)
    for copy in sib_copies():
        copy.wait_recv()
    spread(kpack[0], 1)
    run(0, keys_ref, kdup.at[0], keys.at[0], kdup.at[1])

    for c in range(CHUNKS):
        for copy in part_copies(c):
            copy.wait_recv()
        for copy in fwd_copies(c):
            copy.start()
    spread(kpack[1], 2)
    for c in range(CHUNKS):
        for copy in fwd_copies(c):
            copy.wait_recv()
    spread(kpack[2], 3)
    run(HALF, keys.at[1], kdup.at[2], keys.at[2], kdup.at[3])

    for x in range(tok):
        if x % HALF:
            answer_copy(x).wait_recv()
    for t in range(tok):
        out_ref[t] = answers[target_ref[t]]
    for copy in sib_copies():
        copy.wait_send()
    for c in range(CHUNKS):
        for copy in part_copies(c) + fwd_copies(c):
            copy.wait_send()
    for x in range(tok):
        if x % HALF:
            for copy in query_copies(x):
                copy.wait_send()
            answer_copy(x).wait_send()


def attention(ordering, target, q, rope, new, keys, krope):
    tok, rows, lat = q.shape
    heads, lanes = rope.shape[1:]
    half_len = keys.shape[0]
    packed_len = krope.shape[0]
    bf = jnp.bfloat16
    vmem = pl.BlockSpec(memory_space=pltpu.VMEM)
    smem = pl.BlockSpec(memory_space=pltpu.SMEM)
    dma = pltpu.SemaphoreType.DMA
    return pl.pallas_call(
        attend_kernel,
        out_shape=jax.ShapeDtypeStruct(q.shape, bf),
        in_specs=[smem, smem] + [vmem] * 5,
        out_specs=vmem,
        scratch_shapes=[
            pltpu.VMEM(q.shape, bf),
            pltpu.VMEM(rope.shape, bf),
            pltpu.VMEM(new.shape, bf),
            pltpu.VMEM(q.shape, bf),
            pltpu.VMEM(rope.shape, bf),
            pltpu.VMEM(new.shape, bf),
            pltpu.VMEM((3, half_len, lat), bf),
            pltpu.VMEM((3, packed_len, lanes), bf),
            pltpu.VMEM((4, half_len, lanes), bf),
            pltpu.VMEM(q.shape, bf),
            pltpu.VMEM(q.shape, bf),
            dma((2,)),
            dma((2,)),
            dma((2, CHUNKS)),
            dma((2, CHUNKS)),
            dma((2, CHUNKS)),
            dma((2, CHUNKS)),
            dma((3, tok)),
            dma((3, tok)),
            dma((tok,)),
            dma((tok,)),
        ],
        compiler_params=pltpu.CompilerParams(
            collective_id=0, has_side_effects=True, vmem_limit_bytes=56 * 1024 * 1024
        ),
    )(ordering, target, q, rope, new, keys, krope)


def on_device(
    latent_cache,
    rope_cache,
    q_latent,
    q_rope,
    new_latent,
    new_rope,
    branch_slot,
    moe_input,
    routes,
    route_gate,
    w_gate,
    w_up,
    w_down,
):
    tok_rows, step_count, head_count, lat = q_latent.shape
    rope_width = new_rope.shape[-1]

    model_width = moe_input.shape[-1]
    tok_total = tok_rows * step_count
    expert_count = lax.axis_size("branch") * lax.axis_size("expert") // SHARDS
    slots = expert_count * CAP
    flat = routes.reshape(tok_total, -1)
    chosen = (flat[:, :, None] == jnp.arange(expert_count, dtype=jnp.int32)).astype(jnp.float32)
    gate = jnp.sum(chosen * route_gate.reshape(tok_total, -1, 1), axis=1)
    hit = jnp.sum(chosen, axis=1)
    earlier = (jnp.arange(tok_total)[:, None] > jnp.arange(tok_total)[None, :]).astype(jnp.float32)
    position = jnp.sum(earlier[:, :, None] * hit[None], axis=1)
    placing = hit[:, :, None] * (position[:, :, None] == jnp.arange(CAP, dtype=jnp.float32))
    weights = (placing * gate[:, :, None]).reshape(tok_total, slots)
    placing = placing.reshape(tok_total, slots).astype(jnp.bfloat16)
    tokens_flat = moe_input.reshape(tok_total, model_width)
    outgoing = lax.dot_general(
        placing, tokens_flat, (((0,), (0,)), ((), ())), preferred_element_type=jnp.float32
    ).astype(jnp.bfloat16)
    outgoing = outgoing.reshape(expert_count, 1, CAP, model_width)
    copies = jnp.broadcast_to(outgoing, (expert_count, SHARDS, CAP, model_width))
    copies = copies.reshape(expert_count * SHARDS, CAP, model_width)
    arrived = lax.all_to_all(copies, ("branch", "expert"), split_axis=0, concat_axis=0, tiled=True)
    flattened = arrived.reshape(-1, model_width)
    gate_value = jnp.dot(flattened, w_gate[0], preferred_element_type=jnp.float32)
    lifted = jnp.dot(flattened, w_up[0], preferred_element_type=jnp.float32)
    hidden = (jax.nn.silu(gate_value) * lifted).astype(jnp.bfloat16)
    returned = lax.all_to_all(
        jnp.dot(hidden, w_down[0], preferred_element_type=jnp.float32)
        .astype(jnp.bfloat16)
        .reshape(arrived.shape),
        ("branch", "expert"),
        split_axis=0,
        concat_axis=0,
        tiled=True,
    )
    expert_sums = jnp.sum(
        returned.reshape(expert_count, SHARDS, CAP, model_width).astype(jnp.float32), axis=1
    ).reshape(slots, model_width)
    combined = jnp.sum(weights[:, :, None] * expert_sums[None], axis=1)
    moe_out = combined.astype(jnp.bfloat16).reshape(tok_rows, step_count, model_width)

    counting = jnp.arange(tok_rows, dtype=jnp.int32)
    own_index = lax.axis_index("branch") % tok_rows
    target = jnp.bitwise_xor(own_index, branch_slot)
    chooser = (target[None, :] == counting[:, None]).astype(jnp.int32)
    ordering = jnp.sum(chooser * counting[None, :], axis=1)
    rope = q_rope.reshape(tok_rows, step_count, head_count, rope_width)
    rope = rope.transpose(0, 2, 1, 3).reshape(tok_rows, head_count, step_count * rope_width)
    new = jnp.concatenate([new_latent, new_rope, new_rope], axis=-1)
    new = jnp.pad(new, ((0, 0), (0, 8 - step_count), (0, 0)))
    krope = rope_cache[0].reshape(2, -1, rope_width)
    krope = jnp.concatenate([krope[0], krope[1]], axis=-1)
    attended = attention(
        ordering,
        target,
        q_latent.reshape(tok_rows, step_count * head_count, lat),
        rope,
        new,
        latent_cache[0],
        krope,
    )
    attended = attended.reshape(q_latent.shape)
    return (attended, moe_out)


def solution(mesh):
    return jax.shard_map(
        on_device,
        mesh=mesh,
        in_specs=(
            P(("group", "branch"), "expert", None),
            P(("group", "branch"), "expert", None),
            P(("group", "branch", "expert"), None, None, None),
            P(("group", "branch", "expert"), None, None),
            P(("group", "branch", "expert"), None, None),
            P(("group", "branch", "expert"), None, None),
            P(("group", "branch", "expert")),
            P(("group", "branch", "expert"), None, None),
            P(("group", "branch", "expert"), None, None),
            P(("group", "branch", "expert"), None, None),
            P(("branch", "expert"), None, None),
            P(("branch", "expert"), None, None),
            P(("branch", "expert"), None, None),
        ),
        out_specs=(
            P(("group", "branch", "expert"), None, None, None),
            P(("group", "branch", "expert"), None, None),
        ),
        check_vma=False,
    )
```

```python
import functools

import jax
import jax.numpy as jnp
from jax import lax
from jax.experimental import pallas as pl
from jax.experimental.pallas import tpu as pltpu
from jax.sharding import PartitionSpec as P

SHARDS = 8
CAP = 2
HALF = 4
CHUNKS = 4

softmax_scale = 192.0 ** (-0.5)


def flipped(r, x, bits):
    out = r - r % (1 << bits)
    for j in range(bits):
        out = out + (((r // (1 << j)) + (x // (1 << j))) % 2) * (1 << j)
    return out


def attend_kernel(
    ordering_ref,
    q_ref,
    rope_ref,
    new_ref,
    keys_ref,
    krope_ref,
    blocks_ref,
    w_gate_ref,
    w_up_ref,
    w_down_ref,
    answers,
    sums_ref,
    q_send,
    rope_send,
    new_send,
    q_in,
    rope_in,
    new_in,
    keys,
    kpack,
    kdup,
    result,
    w_gate,
    w_up,
    w_down,
    cross_in,
    mixed,
    mixed_in,
    sib_mixed,
    stacked,
    part_out,
    part_in,
    pair_sum,
    pair_in,
    final,
    load_sem,
    local_sem,
    cross_send,
    cross_recv,
    mix_send,
    mix_recv,
    mixsib_send,
    mixsib_recv,
    y_send,
    y_recv,
    pair_send,
    pair_recv,
    ret_send,
    ret_recv,
    sib_send,
    sib_recv,
    part_send,
    part_recv,
    fwd_send,
    fwd_recv,
    query_send,
    query_recv,
    ans_send,
    ans_recv,
):
    branch = lax.axis_index("branch")
    core = lax.axis_index("expert")
    tok = q_ref.shape[0]
    rows = q_ref.shape[1]
    half_len = keys_ref.shape[0]
    packed_len = krope_ref.shape[0]
    heads = rope_ref.shape[1]
    lanes = rope_ref.shape[2]
    step_rows = half_len // CHUNKS
    pack_rows = packed_len // CHUNKS

    def place(b, c):
        return {"branch": b, "expert": c}

    sibling = place(branch, 1 - core)
    partner = place(flipped(branch, HALF, 3), core)

    def peer(x):
        return place(flipped(branch, x % HALF, 3), core)

    experts = blocks_ref.shape[0]
    block_rows = blocks_ref.shape[1]
    mine = branch // HALF

    def across(d):
        return (mine + d) % experts

    def far(d):
        return place(across(d) * HALF + branch % HALF, core)

    loads = [
        pltpu.make_async_copy(src, dst, load_sem.at[i])
        for i, (src, dst) in enumerate(
            [(w_gate_ref, w_gate), (w_up_ref, w_up), (w_down_ref, w_down)]
        )
    ]
    for copy in loads:
        copy.start()
    barrier = pltpu.get_barrier_semaphore()
    for other in (
        [sibling] + [peer(j) for j in range(1, HALF)] + [far(d) for d in range(1, experts)]
    ):
        pl.semaphore_signal(
            barrier, inc=1, device_id=other, device_id_type=pl.DeviceIdType.MESH
        )
    pl.semaphore_wait(barrier, HALF + experts - 1)

    def remote(src, dst, send, recv, where):
        return pltpu.make_async_remote_copy(
            src_ref=src,
            dst_ref=dst,
            send_sem=send,
            recv_sem=recv,
            device_id=where,
            device_id_type=pl.DeviceIdType.MESH,
        )

    def sib_copies():
        return [
            remote(keys_ref, keys.at[0], sib_send.at[0], sib_recv.at[0], sibling),
            remote(krope_ref, kpack.at[0], sib_send.at[1], sib_recv.at[1], sibling),
        ]

    def part_copies(c):
        big = pl.ds(c * step_rows, step_rows)
        small = pl.ds(c * pack_rows, pack_rows)
        return [
            remote(
                keys_ref.at[big], keys.at[1, big], part_send.at[0, c], part_recv.at[0, c], partner
            ),
            remote(
                krope_ref.at[small],
                kpack.at[1, small],
                part_send.at[1, c],
                part_recv.at[1, c],
                partner,
            ),
        ]

    def fwd_copies(c):
        big = pl.ds(c * step_rows, step_rows)
        small = pl.ds(c * pack_rows, pack_rows)
        return [
            remote(
                keys.at[1, big], keys.at[2, big], fwd_send.at[0, c], fwd_recv.at[0, c], sibling
            ),
            remote(
                kpack.at[1, small], kpack.at[2, small], fwd_send.at[1, c], fwd_recv.at[1, c], sibling
            ),
        ]

    def query_copies(x):
        where = peer(x)
        return [
            remote(q_send.at[x], q_in.at[x], query_send.at[0, x], query_recv.at[0, x], where),
            remote(rope_send.at[x], rope_in.at[x], query_send.at[1, x], query_recv.at[1, x], where),
            remote(new_send.at[x], new_in.at[x], query_send.at[2, x], query_recv.at[2, x], where),
        ]

    def answer_copy(x):
        return remote(result.at[x], answers.at[x], ans_send.at[x], ans_recv.at[x], peer(x))

    def cross_copy(d):
        return remote(
            blocks_ref.at[across(d)], cross_in.at[d], cross_send.at[d], cross_recv.at[d], far(d)
        )

    def mix_copy(j):
        return remote(mixed, mixed_in.at[j], mix_send.at[j], mix_recv.at[j], peer(j))

    def mixsib_copy(j):
        source = mixed if j == 0 else mixed_in.at[j]
        return remote(source, sib_mixed.at[j], mixsib_send.at[j], mixsib_recv.at[j], sibling)

    def y_copy(j):
        return remote(part_out.at[j], part_in.at[j], y_send.at[j], y_recv.at[j], sibling)

    def pair_copy(j):
        return remote(pair_sum.at[j], pair_in.at[j], pair_send.at[j], pair_recv.at[j], peer(j))

    def ret_copy(d):
        return remote(final, sums_ref.at[mine], ret_send.at[d], ret_recv.at[d], far(d))

    own_sums = pltpu.make_async_copy(final, sums_ref.at[mine], local_sem.at[2])

    def mix_blocks():
        total = blocks_ref[mine].astype(jnp.float32)
        for d in range(1, experts):
            cross_copy(d).wait_recv()
            total = total + cross_in[d].astype(jnp.float32)
        mixed[...] = total.astype(jnp.bfloat16)
        for j in (2, 3, 1):
            mix_copy(j).start()

    def share_blocks():
        mixsib_copy(0).start()
        for j in range(1, HALF):
            mix_copy(j).wait_recv()
            mixsib_copy(j).start()

    def feed_forward():
        for j in range(0, HALF):
            mixsib_copy(j).wait_recv()
        for copy in loads:
            copy.wait()
        pieces = [mixed[...]] + [mixed_in[j] for j in range(1, HALF)]
        pieces = pieces + [sib_mixed[j] for j in range(HALF)]
        for i in range(0, 2 * HALF, 2):
            two = jnp.concatenate([p.astype(jnp.float32) for p in pieces[i : i + 2]], axis=0)
            stacked[pl.ds(i * block_rows, 2 * block_rows)] = two.astype(jnp.bfloat16)
        gate = jnp.dot(stacked[...], w_gate[...], preferred_element_type=jnp.float32)
        lifted = jnp.dot(stacked[...], w_up[...], preferred_element_type=jnp.float32)
        hidden = (gate / (1.0 + jnp.exp(-gate)) * lifted).astype(jnp.bfloat16)
        parts = jnp.dot(hidden, w_down[...], preferred_element_type=jnp.float32)
        for j in range(HALF):
            own_at, sib_at = j * block_rows, (HALF + j) * block_rows
            pair_sum[j] = parts[own_at : own_at + block_rows].astype(jnp.bfloat16)
            part_out[j] = parts[sib_at : sib_at + block_rows].astype(jnp.bfloat16)
            y_copy(j).start()

    def add_pairs():
        for j in (2, 3, 1, 0):
            y_copy(j).wait_recv()
            pair_sum[j] = (
                pair_sum[j].astype(jnp.float32) + part_in[j].astype(jnp.float32)
            ).astype(jnp.bfloat16)
            if j:
                pair_copy(j).start()

    def finish_sums():
        total = pair_sum[0].astype(jnp.float32)
        for j in range(1, HALF):
            pair_copy(j).wait_recv()
            total = total + pair_in[j].astype(jnp.float32)
        final[...] = total.astype(jnp.bfloat16)
        own_sums.start()
        for d in range(1, experts):
            ret_copy(d).start()

    def gather(x, to_q, to_rope, to_new):
        at = ordering_ref[x]
        to_q[x] = q_ref[at]
        to_rope[x] = rope_ref[at]
        to_new[x] = new_ref[at]

    for d in range(1, experts):
        cross_copy(d).start()
    for copy in sib_copies():
        copy.start()
    order = [2, 3, 6, 7]
    for c in range(CHUNKS):
        for copy in part_copies(c):
            copy.start()
        x = order[c]
        gather(x, q_send, rope_send, new_send)
        for copy in query_copies(x):
            copy.start()
        if c % 2 == 0:
            y = (1, 5)[c // 2]
            gather(y, q_send, rope_send, new_send)
            for copy in query_copies(y):
                copy.start()
        if c == 1:
            mix_blocks()
    for x in (0, HALF):
        gather(x, q_in, rope_in, new_in)

    lane = lax.broadcasted_iota(jnp.int32, (packed_len, lanes), 1)
    low = lane < lanes // 2

    def spread(packed, slot):
        values = packed.astype(jnp.float32)
        turned = pltpu.roll(values, lanes // 2, 1)
        kdup[slot, pl.ds(0, packed_len)] = jnp.where(low, values, turned).astype(jnp.bfloat16)
        kdup[slot, pl.ds(packed_len, packed_len)] = jnp.where(low, turned, values).astype(
            jnp.bfloat16
        )

    nt = (((1,), (1,)), ((), ()))
    nn = (((1,), (0,)), ((), ()))
    head_low = lax.broadcasted_iota(jnp.int32, (heads, lanes), 1) < lanes // 2
    second = lax.broadcasted_iota(jnp.int32, (rows, 1), 0) >= heads

    def attend(x, first_keys, first_rope, other_keys, other_rope):
        q = q_in[x]
        packed = rope_in[x].astype(jnp.float32)
        qr = jnp.concatenate(
            [jnp.where(head_low, packed, 0.0), jnp.where(head_low, 0.0, packed)], axis=0
        ).astype(jnp.bfloat16)
        fresh = new_in[x]
        lat = q.shape[1]

        def score(k, kr):
            return lax.dot_general(
                q, k, nt, preferred_element_type=jnp.float32
            ) + lax.dot_general(qr, kr, nt, preferred_element_type=jnp.float32)

        own = score(fresh[:, :lat], fresh[:, lat:])
        own0 = own[:, 0:1]
        own1 = jnp.where(second, own[:, 1:2], -1e30)
        s0 = score(first_keys[...], first_rope[...])
        s1 = score(other_keys[...], other_rope[...])
        top = jnp.maximum(jnp.max(s0, axis=1, keepdims=True), jnp.max(s1, axis=1, keepdims=True))
        top = jnp.maximum(top, jnp.maximum(own0, own1))
        p0 = jnp.exp((s0 - top) * softmax_scale)
        p1 = jnp.exp((s1 - top) * softmax_scale)
        w0 = jnp.exp((own0 - top) * softmax_scale)
        w1 = jnp.where(second, jnp.exp((own1 - top) * softmax_scale), 0.0)
        total = jnp.sum(p0, axis=1, keepdims=True) + jnp.sum(p1, axis=1, keepdims=True) + w0 + w1
        summed = lax.dot_general(
            p0.astype(jnp.bfloat16), first_keys[...], nn, preferred_element_type=jnp.float32
        ) + lax.dot_general(
            p1.astype(jnp.bfloat16), other_keys[...], nn, preferred_element_type=jnp.float32
        )
        entries = fresh[:, :lat].astype(jnp.float32)
        summed = summed + w0 * entries[0:1] + w1 * entries[1:2]
        return (summed / total).astype(jnp.bfloat16)

    def local_copy(i):
        return pltpu.make_async_copy(result.at[i * HALF], answers.at[i * HALF], local_sem.at[i])

    def run_local(i, *cache):
        result[i * HALF] = attend(i * HALF, *cache)
        local_copy(i).start()

    def run(start, stop, *cache):
        def body(x, carry):
            for copy in query_copies(x):
                copy.wait_recv()
            result[x] = attend(x, *cache)
            answer_copy(x).start()
            return carry

        lax.fori_loop(start, stop, body, 0)

    spread(krope_ref[...], 0)
    for copy in sib_copies():
        copy.wait_recv()
    spread(kpack[0], 1)
    near = (keys_ref, kdup.at[0], keys.at[0], kdup.at[1])
    run_local(0, *near)
    share_blocks()
    run(1, HALF, *near)
    feed_forward()
    add_pairs()
    finish_sums()

    for c in range(CHUNKS):
        for copy in part_copies(c):
            copy.wait_recv()
        for copy in fwd_copies(c):
            copy.start()
    spread(kpack[1], 2)
    for c in range(CHUNKS):
        for copy in fwd_copies(c):
            copy.wait_recv()
    spread(kpack[2], 3)
    distant = (keys.at[1], kdup.at[2], keys.at[2], kdup.at[3])
    run(HALF + 1, 2 * HALF, *distant)
    run_local(1, *distant)

    for x in range(tok):
        if x % HALF:
            answer_copy(x).wait_recv()
    for d in range(1, experts):
        ret_copy(d).wait_recv()
    own_sums.wait()
    for i in range(2):
        local_copy(i).wait()
    for d in range(1, experts):
        cross_copy(d).wait_send()
        ret_copy(d).wait_send()
    for j in range(HALF):
        mixsib_copy(j).wait_send()
        y_copy(j).wait_send()
        if j:
            mix_copy(j).wait_send()
            pair_copy(j).wait_send()
    for copy in sib_copies():
        copy.wait_send()
    for c in range(CHUNKS):
        for copy in part_copies(c) + fwd_copies(c):
            copy.wait_send()
    for x in range(tok):
        if x % HALF:
            for copy in query_copies(x):
                copy.wait_send()
            answer_copy(x).wait_send()


def attention(ordering, q, rope, new, keys, krope, blocks, w_gate, w_up, w_down):
    tok, rows, lat = q.shape
    heads, lanes = rope.shape[1:]
    half_len = keys.shape[0]
    packed_len = krope.shape[0]
    bf = jnp.bfloat16
    vmem = pl.BlockSpec(memory_space=pltpu.VMEM)
    smem = pl.BlockSpec(memory_space=pltpu.SMEM)
    anywhere = pl.BlockSpec(memory_space=pl.ANY)
    dma = pltpu.SemaphoreType.DMA
    experts, block_rows, width = blocks.shape
    quad = pltpu.VMEM((HALF, block_rows, width), bf)
    block = pltpu.VMEM((block_rows, width), bf)
    return pl.pallas_call(
        attend_kernel,
        out_shape=(jax.ShapeDtypeStruct(q.shape, bf), jax.ShapeDtypeStruct(blocks.shape, bf)),
        in_specs=[smem] + [vmem] * 6 + [anywhere] * 3,
        out_specs=(anywhere, anywhere),
        scratch_shapes=[
            pltpu.VMEM(q.shape, bf),
            pltpu.VMEM(rope.shape, bf),
            pltpu.VMEM(new.shape, bf),
            pltpu.VMEM(q.shape, bf),
            pltpu.VMEM(rope.shape, bf),
            pltpu.VMEM(new.shape, bf),
            pltpu.VMEM((3, half_len, lat), bf),
            pltpu.VMEM((3, packed_len, lanes), bf),
            pltpu.VMEM((4, half_len, lanes), bf),
            pltpu.VMEM(q.shape, bf),
            pltpu.VMEM(w_gate.shape, bf),
            pltpu.VMEM(w_up.shape, bf),
            pltpu.VMEM(w_down.shape, bf),
            pltpu.VMEM((experts, block_rows, width), bf),
            block,
            quad,
            quad,
            pltpu.VMEM((2 * HALF * block_rows, width), bf),
            quad,
            quad,
            quad,
            quad,
            block,
            dma((3,)),
            dma((3,)),
            dma((experts,)),
            dma((experts,)),
            dma((HALF,)),
            dma((HALF,)),
            dma((HALF,)),
            dma((HALF,)),
            dma((HALF,)),
            dma((HALF,)),
            dma((HALF,)),
            dma((HALF,)),
            dma((experts,)),
            dma((experts,)),
            dma((2,)),
            dma((2,)),
            dma((2, CHUNKS)),
            dma((2, CHUNKS)),
            dma((2, CHUNKS)),
            dma((2, CHUNKS)),
            dma((3, tok)),
            dma((3, tok)),
            dma((tok,)),
            dma((tok,)),
        ],
        compiler_params=pltpu.CompilerParams(
            collective_id=0, has_side_effects=True, vmem_limit_bytes=56 * 1024 * 1024
        ),
    )(ordering, q, rope, new, keys, krope, blocks, w_gate, w_up, w_down)


def reorder_kernel(target_ref, source, out, held, read, write):
    tok = held.shape[0]

    def reading(t):
        return pltpu.make_async_copy(source.at[target_ref[t]], held.at[t], read.at[t])

    def writing(t):
        return pltpu.make_async_copy(held.at[t], out.at[t], write.at[t])

    for t in range(tok):
        reading(t).start()
    for t in range(tok):
        reading(t).wait()
        writing(t).start()
    for t in range(tok):
        writing(t).wait()


def reordered(target, source):
    anywhere = pl.BlockSpec(memory_space=pl.ANY)
    tok = source.shape[0]
    return pl.pallas_call(
        reorder_kernel,
        out_shape=jax.ShapeDtypeStruct(source.shape, source.dtype),
        in_specs=[pl.BlockSpec(memory_space=pltpu.SMEM), anywhere],
        out_specs=anywhere,
        scratch_shapes=[
            pltpu.VMEM(source.shape, source.dtype),
            pltpu.SemaphoreType.DMA((tok,)),
            pltpu.SemaphoreType.DMA((tok,)),
        ],
    )(target, source)


def on_device(
    latent_cache,
    rope_cache,
    q_latent,
    q_rope,
    new_latent,
    new_rope,
    branch_slot,
    moe_input,
    routes,
    route_gate,
    w_gate,
    w_up,
    w_down,
):
    tok_rows, step_count, head_count, lat = q_latent.shape
    rope_width = new_rope.shape[-1]

    model_width = moe_input.shape[-1]
    tok_total = tok_rows * step_count
    expert_count = lax.axis_size("branch") * lax.axis_size("expert") // SHARDS
    block_rows = -(-expert_count * CAP // 8) * 8
    flat = routes.reshape(tok_total, -1)
    chosen = (flat[:, :, None] == jnp.arange(expert_count, dtype=jnp.int32)).astype(jnp.float32)
    gate = jnp.sum(chosen * route_gate.reshape(tok_total, -1, 1), axis=1)
    hit = jnp.sum(chosen, axis=1)
    earlier = (jnp.arange(tok_total)[:, None] > jnp.arange(tok_total)[None, :]).astype(jnp.float32)
    position = jnp.sum(earlier[:, :, None] * hit[None], axis=1)
    slot = jnp.arange(block_rows) - CAP * (lax.axis_index("branch") // HALF)
    placing = hit[:, :, None] * (position[:, :, None] == slot.astype(jnp.float32))
    weights = (placing * gate[:, :, None]).reshape(tok_total, -1)
    placing = placing.reshape(tok_total, -1).astype(jnp.bfloat16)
    blocks = (
        lax.dot_general(
            placing,
            moe_input.reshape(tok_total, model_width),
            (((0,), (0,)), ((), ())),
            preferred_element_type=jnp.float32,
        )
        .astype(jnp.bfloat16)
        .reshape(expert_count, block_rows, model_width)
    )

    counting = jnp.arange(tok_rows, dtype=jnp.int32)
    own_index = lax.axis_index("branch") % tok_rows
    target = jnp.bitwise_xor(own_index, branch_slot)
    chooser = (target[None, :] == counting[:, None]).astype(jnp.int32)
    ordering = jnp.sum(chooser * counting[None, :], axis=1)
    rope = q_rope.reshape(tok_rows, step_count, head_count, rope_width)
    rope = rope.transpose(0, 2, 1, 3).reshape(tok_rows, head_count, step_count * rope_width)
    new = jnp.concatenate([new_latent, new_rope, new_rope], axis=-1)
    new = jnp.pad(new, ((0, 0), (0, 8 - step_count), (0, 0)))
    krope = rope_cache[0].reshape(2, -1, rope_width)
    krope = jnp.concatenate([krope[0], krope[1]], axis=-1)
    answers, sums = attention(
        ordering,
        q_latent.reshape(tok_rows, step_count * head_count, lat),
        rope,
        new,
        latent_cache[0],
        krope,
        blocks,
        w_gate[0],
        w_up[0],
        w_down[0],
    )
    attended = reordered(target, answers).reshape(q_latent.shape)
    moe_out = lax.dot_general(
        weights,
        sums.reshape(-1, model_width).astype(jnp.float32),
        (((1,), (0,)), ((), ())),
        precision=lax.Precision.HIGHEST,
        preferred_element_type=jnp.float32,
    )
    moe_out = moe_out.astype(jnp.bfloat16).reshape(tok_rows, step_count, model_width)
    return (attended, moe_out)


def solution(mesh):
    return jax.shard_map(
        on_device,
        mesh=mesh,
        in_specs=(
            P(("group", "branch"), "expert", None),
            P(("group", "branch"), "expert", None),
            P(("group", "branch", "expert"), None, None, None),
            P(("group", "branch", "expert"), None, None),
            P(("group", "branch", "expert"), None, None),
            P(("group", "branch", "expert"), None, None),
            P(("group", "branch", "expert")),
            P(("group", "branch", "expert"), None, None),
            P(("group", "branch", "expert"), None, None),
            P(("group", "branch", "expert"), None, None),
            P(("branch", "expert"), None, None),
            P(("branch", "expert"), None, None),
            P(("branch", "expert"), None, None),
        ),
        out_specs=(
            P(("group", "branch", "expert"), None, None, None),
            P(("group", "branch", "expert"), None, None),
        ),
        check_vma=False,
    )
```

```python
import functools

import jax
import jax.numpy as jnp
from jax import lax
from jax.experimental import pallas as pl
from jax.experimental.pallas import tpu as pltpu
from jax.sharding import PartitionSpec as P

SHARDS = 8
CAP = 2
HALF = 4
CHUNKS = 4

softmax_scale = 192.0 ** (-0.5)


def flipped(r, x, bits):
    out = r - r % (1 << bits)
    for j in range(bits):
        out = out + (((r // (1 << j)) + (x // (1 << j))) % 2) * (1 << j)
    return out


def attend_kernel(
    slot_ref,
    q_ref,
    rope_ref,
    new_ref,
    keys_ref,
    krope_ref,
    blocks_ref,
    w_gate_ref,
    w_up_ref,
    w_down_ref,
    answers,
    sums_ref,
    q_send,
    rope_send,
    new_send,
    q_in,
    rope_in,
    new_in,
    keys,
    kpack,
    kdup,
    result,
    w_gate,
    w_up,
    w_down,
    cross_in,
    mixed,
    mixed_in,
    sib_mixed,
    stacked,
    part_own,
    part_out,
    part_in,
    pair_sum,
    pair_in,
    final,
    load_sem,
    local_sem,
    cross_send,
    cross_recv,
    mix_send,
    mix_recv,
    mixsib_send,
    mixsib_recv,
    y_send,
    y_recv,
    pair_send,
    pair_recv,
    ret_send,
    ret_recv,
    sib_send,
    sib_recv,
    part_send,
    part_recv,
    fwd_send,
    fwd_recv,
    query_send,
    query_recv,
    ans_send,
    ans_recv,
):
    branch = lax.axis_index("branch")
    core = lax.axis_index("expert")
    tok = q_ref.shape[0]
    rows = q_ref.shape[1]
    half_len = keys_ref.shape[0]
    packed_len = krope_ref.shape[0]
    heads = rope_ref.shape[1]
    lanes = rope_ref.shape[2]
    step_rows = half_len // CHUNKS
    pack_rows = packed_len // CHUNKS

    def place(b, c):
        return {"branch": b, "expert": c}

    sibling = place(branch, 1 - core)
    partner = place(flipped(branch, HALF, 3), core)

    def peer(x):
        return place(flipped(branch, x % HALF, 3), core)

    experts = blocks_ref.shape[0]
    block_rows = blocks_ref.shape[1]
    mine = branch // HALF

    def across(d):
        return (mine + d) % experts

    def far(d):
        return place(across(d) * HALF + branch % HALF, core)

    loads = [
        pltpu.make_async_copy(src, dst, load_sem.at[i])
        for i, (src, dst) in enumerate(
            [(w_gate_ref, w_gate), (w_up_ref, w_up), (w_down_ref, w_down)]
        )
    ]
    for copy in loads:
        copy.start()
    barrier = pltpu.get_barrier_semaphore()
    for other in (
        [sibling] + [peer(j) for j in range(1, HALF)] + [far(d) for d in range(1, experts)]
    ):
        pl.semaphore_signal(
            barrier, inc=1, device_id=other, device_id_type=pl.DeviceIdType.MESH
        )
    pl.semaphore_wait(barrier, HALF + experts - 1)

    def remote(src, dst, send, recv, where):
        return pltpu.make_async_remote_copy(
            src_ref=src,
            dst_ref=dst,
            send_sem=send,
            recv_sem=recv,
            device_id=where,
            device_id_type=pl.DeviceIdType.MESH,
        )

    def sib_copies():
        return [
            remote(keys_ref, keys.at[0], sib_send.at[0], sib_recv.at[0], sibling),
            remote(krope_ref, kpack.at[0], sib_send.at[1], sib_recv.at[1], sibling),
        ]

    def part_copies(c):
        big = pl.ds(c * step_rows, step_rows)
        small = pl.ds(c * pack_rows, pack_rows)
        return [
            remote(
                keys_ref.at[big], keys.at[1, big], part_send.at[0, c], part_recv.at[0, c], partner
            ),
            remote(
                krope_ref.at[small],
                kpack.at[1, small],
                part_send.at[1, c],
                part_recv.at[1, c],
                partner,
            ),
        ]

    def fwd_copies(c):
        big = pl.ds(c * step_rows, step_rows)
        small = pl.ds(c * pack_rows, pack_rows)
        return [
            remote(
                keys.at[1, big], keys.at[2, big], fwd_send.at[0, c], fwd_recv.at[0, c], sibling
            ),
            remote(
                kpack.at[1, small], kpack.at[2, small], fwd_send.at[1, c], fwd_recv.at[1, c], sibling
            ),
        ]

    def query_copies(x):
        where = peer(x)
        return [
            remote(q_send.at[x], q_in.at[x], query_send.at[0, x], query_recv.at[0, x], where),
            remote(rope_send.at[x], rope_in.at[x], query_send.at[1, x], query_recv.at[1, x], where),
            remote(new_send.at[x], new_in.at[x], query_send.at[2, x], query_recv.at[2, x], where),
        ]

    def answer_copy(x):
        return remote(result.at[x], answers.at[x], ans_send.at[x], ans_recv.at[x], peer(x))

    def cross_copy(d):
        return remote(
            blocks_ref.at[across(d)], cross_in.at[d], cross_send.at[d], cross_recv.at[d], far(d)
        )

    def mix_copy(j):
        return remote(mixed, mixed_in.at[j], mix_send.at[j], mix_recv.at[j], peer(j))

    def mixsib_copy(j):
        source = mixed if j == 0 else mixed_in.at[j]
        return remote(source, sib_mixed.at[j], mixsib_send.at[j], mixsib_recv.at[j], sibling)

    def y_copy(j):
        return remote(part_out.at[j], part_in.at[j], y_send.at[j], y_recv.at[j], sibling)

    def pair_copy(j):
        return remote(pair_sum.at[j], pair_in.at[j], pair_send.at[j], pair_recv.at[j], peer(j))

    def ret_copy(d):
        return remote(final.at[d], sums_ref.at[mine], ret_send.at[d], ret_recv.at[d], far(experts - d))

    own_sums = pltpu.make_async_copy(final.at[0], sums_ref.at[mine], local_sem.at[2])

    def mix_blocks():
        mixed[0] = blocks_ref[mine]
        for d in range(1, experts):
            cross_copy(d).wait_recv()
            mixed[d] = cross_in[d]
        for j in (2, 3, 1):
            mix_copy(j).start()

    def share_blocks():
        mixsib_copy(0).start()
        for j in range(1, HALF):
            mix_copy(j).wait_recv()
            mixsib_copy(j).start()

    def feed_forward():
        for j in range(0, HALF):
            mixsib_copy(j).wait_recv()
        for copy in loads:
            copy.wait()
        pieces = [mixed] + [mixed_in.at[j] for j in range(1, HALF)]
        pieces = pieces + [sib_mixed.at[j] for j in range(HALF)]
        rows_of = [p[d].astype(jnp.float32) for p in pieces for d in range(experts)]
        stacked[...] = jnp.concatenate(rows_of, axis=0).astype(jnp.bfloat16)
        gate = jnp.dot(stacked[...], w_gate[...], preferred_element_type=jnp.float32)
        lifted = jnp.dot(stacked[...], w_up[...], preferred_element_type=jnp.float32)
        hidden = (gate / (1.0 + jnp.exp(-gate)) * lifted).astype(jnp.bfloat16)
        parts = jnp.dot(hidden, w_down[...], preferred_element_type=jnp.float32)
        for j in range(HALF):
            for d in range(experts):
                own_at = (j * experts + d) * block_rows
                sib_at = own_at + HALF * experts * block_rows
                part_own[j, d] = parts[own_at : own_at + block_rows]
                part_out[j, d] = parts[sib_at : sib_at + block_rows]
            y_copy(j).start()

    def add_pairs():
        for j in (2, 3, 1, 0):
            y_copy(j).wait_recv()
            part_own[j] = part_own[j] + part_in[j]
            pair_sum[j] = part_own[j].astype(jnp.bfloat16)
            if j:
                pair_copy(j).start()

    def finish_sums():
        total = part_own[0]
        for j in range(1, HALF):
            pair_copy(j).wait_recv()
            total = total + pair_in[j].astype(jnp.float32)
        final[...] = total.astype(jnp.bfloat16)
        own_sums.start()
        for d in range(1, experts):
            ret_copy(d).start()

    def gather(x, to_q, to_rope, to_new):
        want = flipped(branch % tok, x, 3)
        at = 0
        for t in range(tok):
            at = jnp.where(slot_ref[t] == want, t, at)
        to_q[x] = q_ref[at]
        to_rope[x] = rope_ref[at]
        to_new[x] = new_ref[at]

    for d in range(1, experts):
        cross_copy(d).start()
    for copy in sib_copies():
        copy.start()
    order = [2, 3, 6, 7]
    for c in range(CHUNKS):
        for copy in part_copies(c):
            copy.start()
        x = order[c]
        gather(x, q_send, rope_send, new_send)
        for copy in query_copies(x):
            copy.start()
        if c % 2 == 0:
            y = (1, 5)[c // 2]
            gather(y, q_send, rope_send, new_send)
            for copy in query_copies(y):
                copy.start()
        if c == 1:
            mix_blocks()
    for x in (0, HALF):
        gather(x, q_in, rope_in, new_in)

    lane = lax.broadcasted_iota(jnp.int32, (packed_len, lanes), 1)
    low = lane < lanes // 2

    def spread(packed, slot):
        values = packed.astype(jnp.float32)
        turned = pltpu.roll(values, lanes // 2, 1)
        kdup[slot, pl.ds(0, packed_len)] = jnp.where(low, values, turned).astype(jnp.bfloat16)
        kdup[slot, pl.ds(packed_len, packed_len)] = jnp.where(low, turned, values).astype(
            jnp.bfloat16
        )

    nt = (((1,), (1,)), ((), ()))
    nn = (((1,), (0,)), ((), ()))
    head_low = lax.broadcasted_iota(jnp.int32, (heads, lanes), 1) < lanes // 2
    second = lax.broadcasted_iota(jnp.int32, (rows, 1), 0) >= heads

    def attend(x, first_keys, first_rope, other_keys, other_rope):
        q = q_in[x]
        packed = rope_in[x].astype(jnp.float32)
        qr = jnp.concatenate(
            [jnp.where(head_low, packed, 0.0), jnp.where(head_low, 0.0, packed)], axis=0
        ).astype(jnp.bfloat16)
        fresh = new_in[x]
        lat = q.shape[1]

        def score(k, kr):
            return lax.dot_general(
                q, k, nt, preferred_element_type=jnp.float32
            ) + lax.dot_general(qr, kr, nt, preferred_element_type=jnp.float32)

        own = score(fresh[:, :lat], fresh[:, lat:])
        own0 = own[:, 0:1]
        own1 = jnp.where(second, own[:, 1:2], -1e30)
        s0 = score(first_keys[...], first_rope[...])
        s1 = score(other_keys[...], other_rope[...])
        top = jnp.maximum(jnp.max(s0, axis=1, keepdims=True), jnp.max(s1, axis=1, keepdims=True))
        top = jnp.maximum(top, jnp.maximum(own0, own1))
        p0 = jnp.exp((s0 - top) * softmax_scale)
        p1 = jnp.exp((s1 - top) * softmax_scale)
        w0 = jnp.exp((own0 - top) * softmax_scale)
        w1 = jnp.where(second, jnp.exp((own1 - top) * softmax_scale), 0.0)
        total = jnp.sum(p0, axis=1, keepdims=True) + jnp.sum(p1, axis=1, keepdims=True) + w0 + w1
        summed = lax.dot_general(
            p0.astype(jnp.bfloat16), first_keys[...], nn, preferred_element_type=jnp.float32
        ) + lax.dot_general(
            p1.astype(jnp.bfloat16), other_keys[...], nn, preferred_element_type=jnp.float32
        )
        entries = fresh[:, :lat].astype(jnp.float32)
        summed = summed + w0 * entries[0:1] + w1 * entries[1:2]
        return (summed / total).astype(jnp.bfloat16)

    def local_copy(i):
        return pltpu.make_async_copy(result.at[i * HALF], answers.at[i * HALF], local_sem.at[i])

    def run_local(i, *cache):
        result[i * HALF] = attend(i * HALF, *cache)
        local_copy(i).start()

    def run(start, stop, *cache):
        def body(x, carry):
            for copy in query_copies(x):
                copy.wait_recv()
            result[x] = attend(x, *cache)
            answer_copy(x).start()
            return carry

        lax.fori_loop(start, stop, body, 0)

    spread(krope_ref[...], 0)
    for copy in sib_copies():
        copy.wait_recv()
    spread(kpack[0], 1)
    near = (keys_ref, kdup.at[0], keys.at[0], kdup.at[1])
    run_local(0, *near)
    share_blocks()
    run(1, HALF, *near)
    feed_forward()
    add_pairs()

    for c in range(CHUNKS):
        for copy in part_copies(c):
            copy.wait_recv()
        for copy in fwd_copies(c):
            copy.start()
    spread(kpack[1], 2)
    for c in range(CHUNKS):
        for copy in fwd_copies(c):
            copy.wait_recv()
    spread(kpack[2], 3)
    distant = (keys.at[1], kdup.at[2], keys.at[2], kdup.at[3])
    finish_sums()
    run(HALF + 1, 2 * HALF, *distant)
    run_local(1, *distant)

    for x in range(tok):
        if x % HALF:
            answer_copy(x).wait_recv()
    for d in range(1, experts):
        ret_copy(d).wait_recv()
    own_sums.wait()
    for i in range(2):
        local_copy(i).wait()
    for d in range(1, experts):
        cross_copy(d).wait_send()
        ret_copy(d).wait_send()
    for j in range(HALF):
        mixsib_copy(j).wait_send()
        y_copy(j).wait_send()
        if j:
            mix_copy(j).wait_send()
            pair_copy(j).wait_send()
    for copy in sib_copies():
        copy.wait_send()
    for c in range(CHUNKS):
        for copy in part_copies(c) + fwd_copies(c):
            copy.wait_send()
    for x in range(tok):
        if x % HALF:
            for copy in query_copies(x):
                copy.wait_send()
            answer_copy(x).wait_send()


def attention(slots, q, rope, new, keys, krope, blocks, w_gate, w_up, w_down):
    tok, rows, lat = q.shape
    heads, lanes = rope.shape[1:]
    half_len = keys.shape[0]
    packed_len = krope.shape[0]
    bf = jnp.bfloat16
    vmem = pl.BlockSpec(memory_space=pltpu.VMEM)
    smem = pl.BlockSpec(memory_space=pltpu.SMEM)
    anywhere = pl.BlockSpec(memory_space=pl.ANY)
    dma = pltpu.SemaphoreType.DMA
    experts, block_rows, width = blocks.shape
    quad = pltpu.VMEM((HALF, experts, block_rows, width), bf)
    quad_sum = pltpu.VMEM((HALF, experts, block_rows, width), jnp.float32)
    block = pltpu.VMEM((experts, block_rows, width), bf)
    return pl.pallas_call(
        attend_kernel,
        out_shape=(jax.ShapeDtypeStruct(q.shape, bf), jax.ShapeDtypeStruct(blocks.shape, bf)),
        in_specs=[smem] + [vmem] * 6 + [anywhere] * 3,
        out_specs=(anywhere, anywhere),
        scratch_shapes=[
            pltpu.VMEM(q.shape, bf),
            pltpu.VMEM(rope.shape, bf),
            pltpu.VMEM(new.shape, bf),
            pltpu.VMEM(q.shape, bf),
            pltpu.VMEM(rope.shape, bf),
            pltpu.VMEM(new.shape, bf),
            pltpu.VMEM((3, half_len, lat), bf),
            pltpu.VMEM((3, packed_len, lanes), bf),
            pltpu.VMEM((4, half_len, lanes), bf),
            pltpu.VMEM(q.shape, bf),
            pltpu.VMEM(w_gate.shape, bf),
            pltpu.VMEM(w_up.shape, bf),
            pltpu.VMEM(w_down.shape, bf),
            pltpu.VMEM((experts, block_rows, width), bf),
            block,
            quad,
            quad,
            pltpu.VMEM((2 * HALF * experts * block_rows, width), bf),
            quad_sum,
            quad_sum,
            quad_sum,
            quad,
            quad,
            block,
            dma((3,)),
            dma((3,)),
            dma((experts,)),
            dma((experts,)),
            dma((HALF,)),
            dma((HALF,)),
            dma((HALF,)),
            dma((HALF,)),
            dma((HALF,)),
            dma((HALF,)),
            dma((HALF,)),
            dma((HALF,)),
            dma((experts,)),
            dma((experts,)),
            dma((2,)),
            dma((2,)),
            dma((2, CHUNKS)),
            dma((2, CHUNKS)),
            dma((2, CHUNKS)),
            dma((2, CHUNKS)),
            dma((3, tok)),
            dma((3, tok)),
            dma((tok,)),
            dma((tok,)),
        ],
        compiler_params=pltpu.CompilerParams(
            collective_id=0, has_side_effects=True, vmem_limit_bytes=56 * 1024 * 1024
        ),
    )(slots, q, rope, new, keys, krope, blocks, w_gate, w_up, w_down)


def reorder_kernel(slot_ref, source, out, held, read, write):
    tok = held.shape[0]
    own = lax.axis_index("branch") % tok

    def chosen(t):
        at = 0
        for x in range(tok):
            at = jnp.where(slot_ref[t] == flipped(own, x, 3), x, at)
        return at

    def reading(t):
        return pltpu.make_async_copy(source.at[chosen(t)], held.at[t], read.at[t])

    def writing(t):
        return pltpu.make_async_copy(held.at[t], out.at[t], write.at[t])

    for t in range(tok):
        reading(t).start()
    for t in range(tok):
        reading(t).wait()
        writing(t).start()
    for t in range(tok):
        writing(t).wait()


def reordered(slots, source):
    anywhere = pl.BlockSpec(memory_space=pl.ANY)
    tok = source.shape[0]
    return pl.pallas_call(
        reorder_kernel,
        out_shape=jax.ShapeDtypeStruct(source.shape, source.dtype),
        in_specs=[pl.BlockSpec(memory_space=pltpu.SMEM), anywhere],
        out_specs=anywhere,
        scratch_shapes=[
            pltpu.VMEM(source.shape, source.dtype),
            pltpu.SemaphoreType.DMA((tok,)),
            pltpu.SemaphoreType.DMA((tok,)),
        ],
    )(slots, source)


def on_device(
    latent_cache,
    rope_cache,
    q_latent,
    q_rope,
    new_latent,
    new_rope,
    branch_slot,
    moe_input,
    routes,
    route_gate,
    w_gate,
    w_up,
    w_down,
):
    tok_rows, step_count, head_count, lat = q_latent.shape
    rope_width = new_rope.shape[-1]

    model_width = moe_input.shape[-1]
    tok_total = tok_rows * step_count
    expert_count = lax.axis_size("branch") * lax.axis_size("expert") // SHARDS
    flat = routes.reshape(tok_total, -1)
    chosen = (flat[:, :, None] == jnp.arange(expert_count, dtype=jnp.int32)).astype(jnp.float32)
    gate = jnp.sum(chosen * route_gate.reshape(tok_total, -1, 1), axis=1)
    hit = jnp.sum(chosen, axis=1)
    earlier = (jnp.arange(tok_total)[:, None] > jnp.arange(tok_total)[None, :]).astype(jnp.float32)
    position = jnp.sum(earlier[:, :, None] * hit[None], axis=1)
    placing = hit[:, :, None] * (position[:, :, None] == jnp.arange(CAP, dtype=jnp.float32))
    weights = (placing * gate[:, :, None]).reshape(tok_total, -1)
    placing = placing.reshape(tok_total, -1).astype(jnp.bfloat16)
    blocks = (
        lax.dot_general(
            placing,
            moe_input.reshape(tok_total, model_width),
            (((0,), (0,)), ((), ())),
            preferred_element_type=jnp.float32,
        )
        .astype(jnp.bfloat16)
        .reshape(expert_count, CAP, model_width)
    )

    rope = q_rope.reshape(tok_rows, step_count, head_count, rope_width)
    rope = rope.transpose(0, 2, 1, 3).reshape(tok_rows, head_count, step_count * rope_width)
    new = jnp.concatenate([new_latent, new_rope, new_rope], axis=-1)
    new = jnp.pad(new, ((0, 0), (0, 8 - step_count), (0, 0)))
    krope = rope_cache[0].reshape(2, -1, rope_width)
    krope = jnp.concatenate([krope[0], krope[1]], axis=-1)
    answers, sums = attention(
        branch_slot,
        q_latent.reshape(tok_rows, step_count * head_count, lat),
        rope,
        new,
        latent_cache[0],
        krope,
        blocks,
        w_gate[0],
        w_up[0],
        w_down[0],
    )
    attended = reordered(branch_slot, answers).reshape(q_latent.shape)
    moe_out = lax.dot_general(
        weights,
        sums.reshape(-1, model_width).astype(jnp.float32),
        (((1,), (0,)), ((), ())),
        precision=lax.Precision.HIGHEST,
        preferred_element_type=jnp.float32,
    )
    moe_out = moe_out.astype(jnp.bfloat16).reshape(tok_rows, step_count, model_width)
    return (attended, moe_out)


def solution(mesh):
    return jax.shard_map(
        on_device,
        mesh=mesh,
        in_specs=(
            P(("group", "branch"), "expert", None),
            P(("group", "branch"), "expert", None),
            P(("group", "branch", "expert"), None, None, None),
            P(("group", "branch", "expert"), None, None),
            P(("group", "branch", "expert"), None, None),
            P(("group", "branch", "expert"), None, None),
            P(("group", "branch", "expert")),
            P(("group", "branch", "expert"), None, None),
            P(("group", "branch", "expert"), None, None),
            P(("group", "branch", "expert"), None, None),
            P(("branch", "expert"), None, None),
            P(("branch", "expert"), None, None),
            P(("branch", "expert"), None, None),
        ),
        out_specs=(
            P(("group", "branch", "expert"), None, None, None),
            P(("group", "branch", "expert"), None, None),
        ),
        check_vma=False,
    )
```

```python
import functools

import jax
import jax.numpy as jnp
from jax import lax
from jax.experimental import pallas as pl
from jax.experimental.pallas import tpu as pltpu
from jax.sharding import PartitionSpec as P

SHARDS = 8
CAP = 2
HALF = 4
CHUNKS = 4

softmax_scale = 192.0 ** (-0.5)


def flipped(r, x, bits):
    out = r - r % (1 << bits)
    for j in range(bits):
        out = out + (((r // (1 << j)) + (x // (1 << j))) % 2) * (1 << j)
    return out


def attend_kernel(
    slot_ref,
    q_ref,
    rope_ref,
    new_ref,
    keys_ref,
    krope_ref,
    blocks_ref,
    w_gate_ref,
    w_up_ref,
    w_down_ref,
    answers,
    sums_ref,
    q_send,
    rope_send,
    new_send,
    q_in,
    rope_in,
    new_in,
    keys,
    kpack,
    kdup,
    result,
    w_gate,
    w_up,
    w_down,
    cross_in,
    mixed,
    mixed_in,
    sib_mixed,
    stacked,
    part_own,
    part_out,
    part_in,
    pair_sum,
    pair_in,
    final,
    load_sem,
    local_sem,
    cross_send,
    cross_recv,
    mix_send,
    mix_recv,
    mixsib_send,
    mixsib_recv,
    y_send,
    y_recv,
    pair_send,
    pair_recv,
    ret_send,
    ret_recv,
    sib_send,
    sib_recv,
    part_send,
    part_recv,
    fwd_send,
    fwd_recv,
    query_send,
    query_recv,
    ans_send,
    ans_recv,
):
    branch = lax.axis_index("branch")
    core = lax.axis_index("expert")
    tok = q_ref.shape[0]
    rows = q_ref.shape[1]
    half_len = keys_ref.shape[0]
    packed_len = krope_ref.shape[0]
    heads = rope_ref.shape[1]
    lanes = rope_ref.shape[2]
    step_rows = half_len // CHUNKS
    pack_rows = packed_len // CHUNKS

    def place(b, c):
        return {"branch": b, "expert": c}

    sibling = place(branch, 1 - core)
    partner = place(flipped(branch, HALF, 3), core)

    def peer(x):
        return place(flipped(branch, x % HALF, 3), core)

    experts = blocks_ref.shape[0]
    block_rows = blocks_ref.shape[1]
    mine = branch // HALF

    def across(d):
        return (mine + d) % experts

    def far(d):
        return place(across(d) * HALF + branch % HALF, core)

    loads = [
        pltpu.make_async_copy(src, dst, load_sem.at[i])
        for i, (src, dst) in enumerate(
            [(w_gate_ref, w_gate), (w_up_ref, w_up), (w_down_ref, w_down)]
        )
    ]
    for copy in loads:
        copy.start()
    barrier = pltpu.get_barrier_semaphore()
    for other in (
        [sibling] + [peer(j) for j in range(1, HALF)] + [far(d) for d in range(1, experts)]
    ):
        pl.semaphore_signal(
            barrier, inc=1, device_id=other, device_id_type=pl.DeviceIdType.MESH
        )
    pl.semaphore_wait(barrier, HALF + experts - 1)

    def remote(src, dst, send, recv, where):
        return pltpu.make_async_remote_copy(
            src_ref=src,
            dst_ref=dst,
            send_sem=send,
            recv_sem=recv,
            device_id=where,
            device_id_type=pl.DeviceIdType.MESH,
        )

    def sib_copies():
        return [
            remote(keys_ref, keys.at[0], sib_send.at[0], sib_recv.at[0], sibling),
            remote(krope_ref, kpack.at[0], sib_send.at[1], sib_recv.at[1], sibling),
        ]

    def part_copies(c):
        big = pl.ds(c * step_rows, step_rows)
        small = pl.ds(c * pack_rows, pack_rows)
        return [
            remote(
                keys_ref.at[big], keys.at[1, big], part_send.at[0, c], part_recv.at[0, c], partner
            ),
            remote(
                krope_ref.at[small],
                kpack.at[1, small],
                part_send.at[1, c],
                part_recv.at[1, c],
                partner,
            ),
        ]

    def fwd_copies(c):
        big = pl.ds(c * step_rows, step_rows)
        small = pl.ds(c * pack_rows, pack_rows)
        return [
            remote(
                keys.at[1, big], keys.at[2, big], fwd_send.at[0, c], fwd_recv.at[0, c], sibling
            ),
            remote(
                kpack.at[1, small], kpack.at[2, small], fwd_send.at[1, c], fwd_recv.at[1, c], sibling
            ),
        ]

    def query_copies(x):
        where = peer(x)
        return [
            remote(q_send.at[x], q_in.at[x], query_send.at[0, x], query_recv.at[0, x], where),
            remote(rope_send.at[x], rope_in.at[x], query_send.at[1, x], query_recv.at[1, x], where),
            remote(new_send.at[x], new_in.at[x], query_send.at[2, x], query_recv.at[2, x], where),
        ]

    def answer_copy(x):
        return remote(result.at[x], answers.at[x], ans_send.at[x], ans_recv.at[x], peer(x))

    def cross_copy(d):
        return remote(
            blocks_ref.at[across(d)], cross_in.at[d], cross_send.at[d], cross_recv.at[d], far(d)
        )

    def mix_copy(j):
        return remote(mixed, mixed_in.at[j], mix_send.at[j], mix_recv.at[j], peer(j))

    def mixsib_copy(j):
        source = mixed if j == 0 else mixed_in.at[j]
        return remote(source, sib_mixed.at[j], mixsib_send.at[j], mixsib_recv.at[j], sibling)

    def y_copy(j):
        return remote(part_out.at[j], part_in.at[j], y_send.at[j], y_recv.at[j], sibling)

    def pair_copy(j):
        return remote(pair_sum.at[j], pair_in.at[j], pair_send.at[j], pair_recv.at[j], peer(j))

    def ret_copy(d):
        return remote(final.at[d], sums_ref.at[mine], ret_send.at[d], ret_recv.at[d], far(experts - d))

    own_sums = pltpu.make_async_copy(final.at[0], sums_ref.at[mine], local_sem.at[2])

    def mix_blocks():
        mixed[0] = blocks_ref[mine]
        for d in range(1, experts):
            cross_copy(d).wait_recv()
            mixed[d] = cross_in[d]
        for j in (2, 3, 1):
            mix_copy(j).start()

    def share_blocks():
        mixsib_copy(0).start()
        for j in range(1, HALF):
            mix_copy(j).wait_recv()
            mixsib_copy(j).start()

    def feed_forward():
        for j in range(0, HALF):
            mixsib_copy(j).wait_recv()
        for copy in loads:
            copy.wait()
        pieces = [mixed] + [mixed_in.at[j] for j in range(1, HALF)]
        pieces = pieces + [sib_mixed.at[j] for j in range(HALF)]
        rows_of = [p[d].astype(jnp.float32) for p in pieces for d in range(experts)]
        stacked[...] = jnp.concatenate(rows_of, axis=0).astype(jnp.bfloat16)
        gate = jnp.dot(stacked[...], w_gate[...], preferred_element_type=jnp.float32)
        lifted = jnp.dot(stacked[...], w_up[...], preferred_element_type=jnp.float32)
        hidden = (gate / (1.0 + jnp.exp(-gate)) * lifted).astype(jnp.bfloat16)
        parts = jnp.dot(hidden, w_down[...], preferred_element_type=jnp.float32)
        for j in range(HALF):
            for d in range(experts):
                own_at = (j * experts + d) * block_rows
                sib_at = own_at + HALF * experts * block_rows
                part_own[j, d] = parts[own_at : own_at + block_rows]
                part_out[j, d] = parts[sib_at : sib_at + block_rows]
            y_copy(j).start()

    def add_pairs():
        for j in (2, 3, 1, 0):
            y_copy(j).wait_recv()
            part_own[j] = part_own[j] + part_in[j]
            pair_sum[j] = part_own[j].astype(jnp.bfloat16)
            if j:
                pair_copy(j).start()

    def finish_sums():
        total = part_own[0]
        for j in range(1, HALF):
            pair_copy(j).wait_recv()
            total = total + pair_in[j].astype(jnp.float32)
        final[...] = total.astype(jnp.bfloat16)
        own_sums.start()
        for d in range(1, experts):
            ret_copy(d).start()

    def gather(x, to_q, to_rope, to_new):
        want = flipped(branch % tok, x, 3)
        at = 0
        for t in range(tok):
            at = jnp.where(slot_ref[t] == want, t, at)
        to_q[x] = q_ref[at]
        to_rope[x] = rope_ref[at]
        to_new[x] = new_ref[at]

    for d in range(1, experts):
        cross_copy(d).start()
    for copy in sib_copies():
        copy.start()
    order = [2, 3, 6, 7]
    for c in range(CHUNKS):
        for copy in part_copies(c):
            copy.start()
        x = order[c]
        gather(x, q_send, rope_send, new_send)
        for copy in query_copies(x):
            copy.start()
        if c % 2 == 0:
            y = (1, 5)[c // 2]
            gather(y, q_send, rope_send, new_send)
            for copy in query_copies(y):
                copy.start()
        if c == 1:
            mix_blocks()
    for x in (0, HALF):
        gather(x, q_in, rope_in, new_in)

    lane = lax.broadcasted_iota(jnp.int32, (packed_len, lanes), 1)
    low = lane < lanes // 2

    def spread(packed, slot):
        values = packed.astype(jnp.float32)
        turned = pltpu.roll(values, lanes // 2, 1)
        kdup[slot, pl.ds(0, packed_len)] = jnp.where(low, values, turned).astype(jnp.bfloat16)
        kdup[slot, pl.ds(packed_len, packed_len)] = jnp.where(low, turned, values).astype(
            jnp.bfloat16
        )

    nt = (((1,), (1,)), ((), ()))
    nn = (((1,), (0,)), ((), ()))
    head_low = lax.broadcasted_iota(jnp.int32, (heads, lanes), 1) < lanes // 2
    second = lax.broadcasted_iota(jnp.int32, (rows, 1), 0) >= heads

    def attend(x, first_keys, first_rope, other_keys, other_rope):
        q = q_in[x]
        packed = rope_in[x].astype(jnp.float32)
        qr = jnp.concatenate(
            [jnp.where(head_low, packed, 0.0), jnp.where(head_low, 0.0, packed)], axis=0
        ).astype(jnp.bfloat16)
        fresh = new_in[x]
        lat = q.shape[1]

        def score(k, kr):
            return lax.dot_general(
                q, k, nt, preferred_element_type=jnp.float32
            ) + lax.dot_general(qr, kr, nt, preferred_element_type=jnp.float32)

        own = score(fresh[:, :lat], fresh[:, lat:])
        own0 = own[:, 0:1]
        own1 = jnp.where(second, own[:, 1:2], -1e30)
        s0 = score(first_keys[...], first_rope[...])
        s1 = score(other_keys[...], other_rope[...])
        top = jnp.maximum(jnp.max(s0, axis=1, keepdims=True), jnp.max(s1, axis=1, keepdims=True))
        top = jnp.maximum(top, jnp.maximum(own0, own1))
        p0 = jnp.exp((s0 - top) * softmax_scale)
        p1 = jnp.exp((s1 - top) * softmax_scale)
        w0 = jnp.exp((own0 - top) * softmax_scale)
        w1 = jnp.where(second, jnp.exp((own1 - top) * softmax_scale), 0.0)
        total = jnp.sum(p0, axis=1, keepdims=True) + jnp.sum(p1, axis=1, keepdims=True) + w0 + w1
        summed = lax.dot_general(
            p0.astype(jnp.bfloat16), first_keys[...], nn, preferred_element_type=jnp.float32
        ) + lax.dot_general(
            p1.astype(jnp.bfloat16), other_keys[...], nn, preferred_element_type=jnp.float32
        )
        entries = fresh[:, :lat].astype(jnp.float32)
        summed = summed + w0 * entries[0:1] + w1 * entries[1:2]
        return (summed / total).astype(jnp.bfloat16)

    def local_copy(i):
        return pltpu.make_async_copy(result.at[i * HALF], answers.at[i * HALF], local_sem.at[i])

    def run_local(i, *cache):
        result[i * HALF] = attend(i * HALF, *cache)
        local_copy(i).start()

    def run(start, stop, *cache):
        def body(i, carry):
            x = start + (i + 1) % (stop - start)
            for copy in query_copies(x):
                copy.wait_recv()
            result[x] = attend(x, *cache)
            answer_copy(x).start()
            return carry

        lax.fori_loop(0, stop - start, body, 0)

    spread(krope_ref[...], 0)
    for copy in sib_copies():
        copy.wait_recv()
    spread(kpack[0], 1)
    near = (keys_ref, kdup.at[0], keys.at[0], kdup.at[1])
    run_local(0, *near)
    share_blocks()
    run(1, HALF, *near)
    feed_forward()
    add_pairs()

    for c in range(CHUNKS):
        for copy in part_copies(c):
            copy.wait_recv()
        for copy in fwd_copies(c):
            copy.start()
    spread(kpack[1], 2)
    for c in range(CHUNKS):
        for copy in fwd_copies(c):
            copy.wait_recv()
    spread(kpack[2], 3)
    distant = (keys.at[1], kdup.at[2], keys.at[2], kdup.at[3])
    finish_sums()
    run(HALF + 1, 2 * HALF, *distant)
    run_local(1, *distant)

    for x in range(tok):
        if x % HALF:
            answer_copy(x).wait_recv()
    for d in range(1, experts):
        ret_copy(d).wait_recv()
    own_sums.wait()
    for i in range(2):
        local_copy(i).wait()
    for d in range(1, experts):
        cross_copy(d).wait_send()
        ret_copy(d).wait_send()
    for j in range(HALF):
        mixsib_copy(j).wait_send()
        y_copy(j).wait_send()
        if j:
            mix_copy(j).wait_send()
            pair_copy(j).wait_send()
    for copy in sib_copies():
        copy.wait_send()
    for c in range(CHUNKS):
        for copy in part_copies(c) + fwd_copies(c):
            copy.wait_send()
    for x in range(tok):
        if x % HALF:
            for copy in query_copies(x):
                copy.wait_send()
            answer_copy(x).wait_send()


def attention(slots, q, rope, new, keys, krope, blocks, w_gate, w_up, w_down):
    tok, rows, lat = q.shape
    heads, lanes = rope.shape[1:]
    half_len = keys.shape[0]
    packed_len = krope.shape[0]
    bf = jnp.bfloat16
    vmem = pl.BlockSpec(memory_space=pltpu.VMEM)
    smem = pl.BlockSpec(memory_space=pltpu.SMEM)
    anywhere = pl.BlockSpec(memory_space=pl.ANY)
    dma = pltpu.SemaphoreType.DMA
    experts, block_rows, width = blocks.shape
    quad = pltpu.VMEM((HALF, experts, block_rows, width), bf)
    quad_sum = pltpu.VMEM((HALF, experts, block_rows, width), jnp.float32)
    block = pltpu.VMEM((experts, block_rows, width), bf)
    return pl.pallas_call(
        attend_kernel,
        out_shape=(jax.ShapeDtypeStruct(q.shape, bf), jax.ShapeDtypeStruct(blocks.shape, bf)),
        in_specs=[smem] + [vmem] * 6 + [anywhere] * 3,
        out_specs=(anywhere, anywhere),
        scratch_shapes=[
            pltpu.VMEM(q.shape, bf),
            pltpu.VMEM(rope.shape, bf),
            pltpu.VMEM(new.shape, bf),
            pltpu.VMEM(q.shape, bf),
            pltpu.VMEM(rope.shape, bf),
            pltpu.VMEM(new.shape, bf),
            pltpu.VMEM((3, half_len, lat), bf),
            pltpu.VMEM((3, packed_len, lanes), bf),
            pltpu.VMEM((4, half_len, lanes), bf),
            pltpu.VMEM(q.shape, bf),
            pltpu.VMEM(w_gate.shape, bf),
            pltpu.VMEM(w_up.shape, bf),
            pltpu.VMEM(w_down.shape, bf),
            pltpu.VMEM((experts, block_rows, width), bf),
            block,
            quad,
            quad,
            pltpu.VMEM((2 * HALF * experts * block_rows, width), bf),
            quad_sum,
            quad_sum,
            quad_sum,
            quad,
            quad,
            block,
            dma((3,)),
            dma((3,)),
            dma((experts,)),
            dma((experts,)),
            dma((HALF,)),
            dma((HALF,)),
            dma((HALF,)),
            dma((HALF,)),
            dma((HALF,)),
            dma((HALF,)),
            dma((HALF,)),
            dma((HALF,)),
            dma((experts,)),
            dma((experts,)),
            dma((2,)),
            dma((2,)),
            dma((2, CHUNKS)),
            dma((2, CHUNKS)),
            dma((2, CHUNKS)),
            dma((2, CHUNKS)),
            dma((3, tok)),
            dma((3, tok)),
            dma((tok,)),
            dma((tok,)),
        ],
        compiler_params=pltpu.CompilerParams(
            collective_id=0, has_side_effects=True, vmem_limit_bytes=56 * 1024 * 1024
        ),
    )(slots, q, rope, new, keys, krope, blocks, w_gate, w_up, w_down)


def reorder_kernel(slot_ref, source, out, held, read, write):
    tok = held.shape[0]
    own = lax.axis_index("branch") % tok

    def chosen(t):
        at = 0
        for x in range(tok):
            at = jnp.where(slot_ref[t] == flipped(own, x, 3), x, at)
        return at

    def reading(t):
        return pltpu.make_async_copy(source.at[chosen(t)], held.at[t], read.at[t])

    def writing(t):
        return pltpu.make_async_copy(held.at[t], out.at[t], write.at[t])

    for t in range(tok):
        reading(t).start()
    for t in range(tok):
        reading(t).wait()
        writing(t).start()
    for t in range(tok):
        writing(t).wait()


def reordered(slots, source):
    anywhere = pl.BlockSpec(memory_space=pl.ANY)
    tok = source.shape[0]
    return pl.pallas_call(
        reorder_kernel,
        out_shape=jax.ShapeDtypeStruct(source.shape, source.dtype),
        in_specs=[pl.BlockSpec(memory_space=pltpu.SMEM), anywhere],
        out_specs=anywhere,
        scratch_shapes=[
            pltpu.VMEM(source.shape, source.dtype),
            pltpu.SemaphoreType.DMA((tok,)),
            pltpu.SemaphoreType.DMA((tok,)),
        ],
    )(slots, source)


def on_device(
    latent_cache,
    rope_cache,
    q_latent,
    q_rope,
    new_latent,
    new_rope,
    branch_slot,
    moe_input,
    routes,
    route_gate,
    w_gate,
    w_up,
    w_down,
):
    tok_rows, step_count, head_count, lat = q_latent.shape
    rope_width = new_rope.shape[-1]

    model_width = moe_input.shape[-1]
    tok_total = tok_rows * step_count
    expert_count = lax.axis_size("branch") * lax.axis_size("expert") // SHARDS
    flat = routes.reshape(tok_total, -1)
    chosen = (flat[:, :, None] == jnp.arange(expert_count, dtype=jnp.int32)).astype(jnp.float32)
    gate = jnp.sum(chosen * route_gate.reshape(tok_total, -1, 1), axis=1)
    hit = jnp.sum(chosen, axis=1)
    earlier = (jnp.arange(tok_total)[:, None] > jnp.arange(tok_total)[None, :]).astype(jnp.float32)
    position = jnp.sum(earlier[:, :, None] * hit[None], axis=1)
    placing = hit[:, :, None] * (position[:, :, None] == jnp.arange(CAP, dtype=jnp.float32))
    weights = (placing * gate[:, :, None]).reshape(tok_total, -1)
    placing = placing.reshape(tok_total, -1).astype(jnp.bfloat16)
    blocks = (
        lax.dot_general(
            placing,
            moe_input.reshape(tok_total, model_width),
            (((0,), (0,)), ((), ())),
            preferred_element_type=jnp.float32,
        )
        .astype(jnp.bfloat16)
        .reshape(expert_count, CAP, model_width)
    )

    rope = q_rope.reshape(tok_rows, step_count, head_count, rope_width)
    rope = rope.transpose(0, 2, 1, 3).reshape(tok_rows, head_count, step_count * rope_width)
    new = jnp.concatenate([new_latent, new_rope, new_rope], axis=-1)
    new = jnp.pad(new, ((0, 0), (0, 8 - step_count), (0, 0)))
    krope = rope_cache[0].reshape(2, -1, rope_width)
    krope = jnp.concatenate([krope[0], krope[1]], axis=-1)
    answers, sums = attention(
        branch_slot,
        q_latent.reshape(tok_rows, step_count * head_count, lat),
        rope,
        new,
        latent_cache[0],
        krope,
        blocks,
        w_gate[0],
        w_up[0],
        w_down[0],
    )
    attended = reordered(branch_slot, answers).reshape(q_latent.shape)
    moe_out = lax.dot_general(
        weights,
        sums.reshape(-1, model_width).astype(jnp.float32),
        (((1,), (0,)), ((), ())),
        precision=lax.Precision.HIGHEST,
        preferred_element_type=jnp.float32,
    )
    moe_out = moe_out.astype(jnp.bfloat16).reshape(tok_rows, step_count, model_width)
    return (attended, moe_out)


def solution(mesh):
    return jax.shard_map(
        on_device,
        mesh=mesh,
        in_specs=(
            P(("group", "branch"), "expert", None),
            P(("group", "branch"), "expert", None),
            P(("group", "branch", "expert"), None, None, None),
            P(("group", "branch", "expert"), None, None),
            P(("group", "branch", "expert"), None, None),
            P(("group", "branch", "expert"), None, None),
            P(("group", "branch", "expert")),
            P(("group", "branch", "expert"), None, None),
            P(("group", "branch", "expert"), None, None),
            P(("group", "branch", "expert"), None, None),
            P(("branch", "expert"), None, None),
            P(("branch", "expert"), None, None),
            P(("branch", "expert"), None, None),
        ),
        out_specs=(
            P(("group", "branch", "expert"), None, None, None),
            P(("group", "branch", "expert"), None, None),
        ),
        check_vma=False,
    )
```
